1024 devices in a mesh: ctx: 32 (over z_hi, x, core), ch: 32 (over z_lo, y).
Axes of the slice: x: 4, y: 8, z: 16 (z_hi: 4, z_lo: 4; z = z_hi * 4 + z_lo), core: 2. Of those that a mesh axis runs over, the one named last changes fastest.
Arguments:
- value_in: bfloat16 [8192, 16384], P('ch', 'ctx'), may hold values from -6 to 6
- key_in: bfloat16 [8192, 16384], P('ch', 'ctx'), may hold values from -6 to 6
- gate_first: bfloat16 [8192, 16384], P('ch', 'ctx'), may hold values from -6 to 6
- gate_second: bfloat16 [8192, 16384], P('ch', 'ctx'), may hold values from -6 to 6
- gate_long: bfloat16 [8192, 16384], P('ch', 'ctx'), may hold values from -6 to 6
- filter_first: bfloat16 [512, 128], P('ch'), may hold values from -0.5 to 0.5
- filter_second: bfloat16 [512, 128], P('ch'), may hold values from -0.5 to 0.5
- long_filter: bfloat16 [8192, 16384], P(('ch', 'ctx')), may hold values from -0.046875 to 0.046875
- skip_gain: float32 [8192], P('ch'), may hold values from 0.5 to 1.5
Outputs:
- mixed_out: bfloat16 [8192, 16384], P('ch', 'ctx')
The draws below stay inside these ranges and needn't reach their ends.
All inputs are finite; a program needn't handle non-finite values.
Results may differ from the reference program's by a relative error of at most 0.0085.
Values may be sent and summed in bfloat16 or wider, within the bound.
No kernel may reach another device: no remote copies, remote signals or barrier semaphores. Data moves between devices by JAX's collectives and lax.ppermute only.
A program may use at most 32 MiB of HBM per device.

```python
import math
import jax
import jax.numpy as jnp
from jax import lax

D = 8192
CG = 16
TAPS = 128
SEQ = 16384
GROUPS = 512


def level_of(stream_key, extent, shards, least, top_value):
    def one(axis_at, parts):
        heights = jax.random.uniform(jax.random.fold_in(jax.random.fold_in(stream_key, 6), axis_at), (parts,), jnp.float32, least / len(shards), top_value / len(shards))
        return jnp.repeat(jnp.exp(heights), extent[axis_at] // parts).reshape((-1,) + (1,) * (len(extent) - axis_at - 1))

    factor_of = one(*shards[0])
    for cut in shards[1:]:
        factor_of = factor_of * one(*cut)
    return factor_of


def centred(stream_key, extent, width, bound, cuts=(), dtype=jnp.bfloat16):
    gain = level_of(stream_key, extent, cuts, -0.22, 0.18) if cuts else 1.0
    values = jax.random.normal(stream_key, extent, jnp.float32) * width * gain
    return jnp.minimum(jnp.maximum(values, -bound), bound).astype(dtype)


def setup_inputs(seed: int = 0) -> dict:
    arg_keys = jax.random.split(jax.random.key(seed), 10)
    return {
        "value_in": centred(arg_keys[0], (D, SEQ), 1.0, 6.0, ((0, 32), (1, 32))),
        "key_in": centred(arg_keys[1], (D, SEQ), 1.0, 6.0, ((0, 32), (1, 32))),
        "gate_first": centred(arg_keys[2], (D, SEQ), 1.0, 6.0, ((0, 32), (1, 32))),
        "gate_second": centred(arg_keys[3], (D, SEQ), 1.0, 6.0, ((0, 32), (1, 32))),
        "gate_long": centred(arg_keys[4], (D, SEQ), 1.0, 6.0, ((0, 32), (1, 32))),
        "filter_first": centred(arg_keys[5], (GROUPS, TAPS), TAPS ** -0.5, 0.5, ((0, 32),)),
        "filter_second": centred(arg_keys[6], (GROUPS, TAPS), TAPS ** -0.5, 0.5, ((0, 32),)),
        "long_filter": centred(arg_keys[7], (D, SEQ), SEQ ** -0.5, 0.046875, ((0, 1024),)),
        "skip_gain": jnp.clip(0.5 + 1.0 * jax.random.uniform(arg_keys[8], (D,), jnp.float32) ** level_of(arg_keys[8], (D,), ((0, 32),), -0.2, 0.2), 0.5, 1.5),
    }


def causal_conv(signal, filters):
    per_channel = jnp.repeat(filters.astype(jnp.float32), CG, axis=0)
    length = signal.shape[1]
    padded = jnp.pad(signal.astype(jnp.float32), ((0, 0), (TAPS, 0)))

    def add_tap(tap, total):
        weight = lax.dynamic_slice_in_dim(per_channel, tap, 1, 1)
        shifted = lax.dynamic_slice_in_dim(padded, TAPS - tap, length, 1)
        return total + weight * shifted

    return lax.fori_loop(0, TAPS, add_tap, jnp.zeros(signal.shape, jnp.float32))


def long_conv(block_args):
    signal, filt_vals, skip_part = block_args
    length = signal.shape[1]
    spectrum = jnp.fft.rfft(signal, n=2 * length, axis=1) * jnp.fft.rfft(filt_vals, n=2 * length, axis=1)
    convolved = jnp.fft.irfft(spectrum, n=2 * length, axis=1)[:, :length]
    return skip_part[:, None] * signal + convolved


def reference(value_in, key_in, gate_first, gate_second, gate_long, filter_first, filter_second, long_filter, skip_gain):
    mixed_in = (key_in.astype(jnp.float32) * value_in.astype(jnp.float32)).astype(jnp.bfloat16)
    mixed_in = lax.optimization_barrier(mixed_in)
    first_out = (gate_first.astype(jnp.float32) * causal_conv(mixed_in, filter_first)).astype(jnp.bfloat16)
    first_out = lax.optimization_barrier(first_out)
    second_out = (gate_second.astype(jnp.float32) * causal_conv(first_out, filter_second)).astype(jnp.bfloat16)
    second_out = lax.optimization_barrier(second_out)
    block_size = math.gcd(D, 256)
    block_count = D // block_size
    long_out = lax.map(long_conv, (second_out.astype(jnp.float32).reshape(block_count, block_size, SEQ),
                                   long_filter.astype(jnp.float32).reshape(block_count, block_size, SEQ),
                                   skip_gain.reshape(block_count, block_size)))
    long_out = long_out.reshape(D, SEQ).astype(jnp.bfloat16)
    long_out = lax.optimization_barrier(long_out)
    return (gate_long.astype(jnp.float32) * long_out.astype(jnp.float32)).astype(jnp.bfloat16)
```

```python
import functools

import jax
import jax.numpy as jnp
import numpy as np
from jax import lax
from jax.experimental import pallas as pl
from jax.experimental.pallas import tpu as pltpu
from jax.sharding import PartitionSpec as P

SPLIT = False
LANES = 128
VMEM = pl.BlockSpec(memory_space=pltpu.VMEM)
SMEM = pl.BlockSpec(memory_space=pltpu.SMEM)
BF16 = jnp.bfloat16
F32 = jnp.float32


def matmul(a, b):
    return jnp.dot(a, b, preferred_element_type=F32)


def band(taps_ref, group):
    taps = taps_ref[pl.ds(group, 1), :].astype(F32)
    ring = jnp.concatenate([taps, jnp.zeros_like(taps)], axis=1)
    rows = jnp.broadcast_to(ring, (8, 2 * LANES))
    rows = pltpu.roll(rows, LANES, 1, stride=1, stride_axis=0)
    strips = [rows if m == 0 else pltpu.roll(rows, 8 * m, 1) for m in range(LANES // 8)]
    top = jnp.concatenate([s[:, :LANES] for s in strips], axis=0)
    bottom = jnp.concatenate([s[:, LANES:] for s in strips], axis=0)
    return jnp.concatenate([top, bottom], axis=0).astype(BF16)


def conv_blocks(wide, matrix, first, last):
    rows = wide.shape[0]
    stack = jnp.concatenate(
        [wide[:, b * LANES : (b + 2) * LANES] for b in range(first, last)], axis=0
    )
    out = matmul(stack, matrix)
    return jnp.concatenate([out[i * rows : (i + 1) * rows] for i in range(last - first)], axis=1)


def near_kernel(value, key, gate_one, gate_two, taps_one, taps_two, tails, kept, done, matrices):
    groups = taps_one.shape[0]
    rows = value.shape[0] // groups
    length = value.shape[1]
    for g in range(groups):
        at = pl.ds(g * rows, rows)
        matrix_one = band(taps_one, g)
        matrix_two = band(taps_two, g)
        matrices[0, g] = matrix_one
        matrices[1, g] = matrix_two
        mixed = (key[at, :].astype(F32) * value[at, :].astype(F32)).astype(BF16)
        tails[at, :LANES] = mixed[:, length - LANES :]
        first = conv_blocks(mixed, matrix_one, 0, 3)
        first = (gate_one[at, LANES:].astype(F32) * first).astype(BF16)
        tails[at, LANES:] = first[:, 2 * LANES :]
        kept[at, :] = first[:, :LANES]
        second = conv_blocks(first, matrix_two, 0, 2)
        done[at, :] = (gate_two[at, 2 * LANES :].astype(F32) * second).astype(BF16)


def edge_kernel(value, key, gate_one, gate_two, kept, matrices, halo, done, out):
    groups = matrices.shape[1]
    rows = value.shape[0] // groups
    for g in range(groups):
        at = pl.ds(g * rows, rows)
        mixed = (key[at, :].astype(F32) * value[at, :].astype(F32)).astype(BF16)
        mixed = jnp.concatenate([halo[at, :LANES], mixed], axis=1)
        first = conv_blocks(mixed, matrices[0, g], 0, 1)
        first = (gate_one[at, :].astype(F32) * first).astype(BF16)
        first = jnp.concatenate([halo[at, LANES:], first, kept[at, :]], axis=1)
        second = conv_blocks(first, matrices[1, g], 0, 2)
        second = (gate_two[at, :].astype(F32) * second).astype(BF16)
        out[at, : 2 * LANES] = second
        if not SPLIT:
            out[at, 2 * LANES :] = done[at, :]


def tables(length, devices):
    n = LANES
    per = length // n // devices
    order = np.arange(n)
    n1 = (order % devices) * per + order // devices
    k1 = np.arange(n) + 0.25
    outer = 2 * np.pi * np.outer(k1, n1) / n
    outer_table = np.concatenate([np.cos(outer), -np.sin(outer)], axis=0)
    inner = 2 * np.pi * np.outer(np.arange(n), np.arange(n)) / n
    cos, sin = np.cos(inner), np.sin(inner)
    ahead = np.block([[cos, -sin], [sin, cos]])
    back = np.block([[cos, sin], [-sin, cos]])
    turn = 2 * np.pi * np.outer(k1, np.arange(n)) / length
    half = lambda t: jnp.asarray(t, F32).astype(BF16)
    return (
        half(outer_table),
        half(outer_table.T),
        half(ahead),
        half(back),
        jnp.asarray(np.cos(turn), F32),
        jnp.asarray(np.sin(turn), F32),
    )


def transform(values, outer, ahead, cos, sin):
    n = LANES
    parts = matmul(outer[...], values)
    re, im = parts[:n], parts[n:]
    turned = jnp.concatenate([re * cos + im * sin, im * cos - re * sin], axis=1)
    return matmul(turned.astype(BF16), ahead[...])


def filter_kernel(devices, taps, outer, ahead, cos, sin, spectrum, rows):
    channels, length = taps.shape
    n = LANES
    per = length // n // devices
    scale = 1.0 / length
    for b in range(length // n):
        place = (b % per) * devices + b // per
        rows[pl.ds(place * channels, channels), :] = taps[:, b * n : (b + 1) * n].astype(F32)
    for c in range(channels):
        values = rows[pl.ds(c, n, stride=channels), :].astype(BF16)
        spectrum[c] = transform(values, outer, ahead, cos[...], sin[...]) * scale


def long_kernel(*refs):
    if SPLIT:
        late, early, spectrum, skip, outer, outer_t, ahead, back, cos, sin, out, rows, outs = refs
    else:
        early, spectrum, skip, outer, outer_t, ahead, back, cos, sin, out, rows, outs = refs
    n = LANES
    devices, channels, length = out.shape
    for part, piece in enumerate((early, late) if SPLIT else (early,)):
        width = piece.shape[2]
        flat = piece[...].astype(F32).reshape(devices * channels, width)
        for q in range(width // n):
            rows[part * (width // n) + q] = flat[:, q * n : (q + 1) * n]
    base = lax.axis_index("ctx") * channels
    cosines, sines = cos[...], sin[...]
    for c in range(channels):
        signal = jnp.concatenate(
            [
                rows[q, pl.ds(c, devices, stride=channels), :]
                for q in range(length // n)
            ],
            axis=0,
        )
        waves = transform(signal.astype(BF16), outer, ahead, cosines, sines)
        re, im = waves[:, :n], waves[:, n:]
        filter_re, filter_im = spectrum[c, :, :n], spectrum[c, :, n:]
        product = jnp.concatenate(
            [re * filter_re - im * filter_im, re * filter_im + im * filter_re], axis=1
        )
        waves = matmul(product.astype(BF16), back[...])
        re, im = waves[:, :n], waves[:, n:]
        turned = jnp.concatenate([re * cosines - im * sines, re * sines + im * cosines], axis=0)
        result = matmul(outer_t[...], turned.astype(BF16)) + skip[base + c] * signal
        for q in range(length // n):
            outs[q, pl.ds(c, devices, stride=channels), :] = result[
                q * devices : (q + 1) * devices
            ]
    for q in range(length // n):
        block = outs[q].reshape(devices, channels, n)
        out[:, :, q * n : (q + 1) * n] = block.astype(BF16)


def shards(
    value_in,
    key_in,
    gate_first,
    gate_second,
    gate_long,
    filter_first,
    filter_second,
    long_filter,
    skip_gain,
):
    channels, length = value_in.shape
    devices = lax.axis_size("ctx")
    per = channels // devices
    groups = filter_first.shape[0]
    total = length * devices
    half = length // 2
    shape = jax.ShapeDtypeStruct

    tails, kept, late, matrices = pl.pallas_call(
        near_kernel,
        out_shape=(
            shape((channels, 2 * LANES), BF16),
            shape((channels, LANES), BF16),
            shape((channels, half), BF16),
            shape((2, groups, 2 * LANES, LANES), BF16),
        ),
        in_specs=[VMEM] * 6,
        out_specs=(VMEM,) * 4,
        name="near",
    )(value_in, key_in, gate_first, gate_second, filter_first, filter_second)
    halo = lax.ppermute(tails, "ctx", [(i, i + 1) for i in range(devices - 1)])

    outer, outer_t, ahead, back, cos, sin = tables(total, devices)
    spectrum = pl.pallas_call(
        functools.partial(filter_kernel, devices),
        out_shape=shape((per, LANES, 2 * LANES), F32),
        in_specs=[VMEM] * 5,
        out_specs=VMEM,
        scratch_shapes=[pltpu.VMEM((LANES * per, LANES), F32)],
        name="spectrum",
    )(long_filter, outer, ahead, cos, sin)

    width = half if SPLIT else length
    early = pl.pallas_call(
        edge_kernel,
        out_shape=shape((channels, width), BF16),
        grid=(1,),
        in_specs=[
            pl.BlockSpec((channels, half), lambda i: (0, 0)),
            pl.BlockSpec((channels, half), lambda i: (0, 0)),
            pl.BlockSpec((channels, LANES), lambda i: (0, 0)),
            pl.BlockSpec((channels, half), lambda i: (0, 0)),
            VMEM,
            VMEM,
            VMEM,
            VMEM,
        ],
        out_specs=VMEM,
        name="edge",
    )(value_in, key_in, gate_first, gate_second, kept, matrices, halo, late)

    def swap(data):
        return lax.all_to_all(data, "ctx", split_axis=0, concat_axis=0, tiled=True)

    moved = [swap(early.reshape(devices, per, width))]
    if SPLIT:
        moved = [swap(late.reshape(devices, per, half))] + moved
    long_out = pl.pallas_call(
        long_kernel,
        out_shape=shape((devices, per, length), BF16),
        in_specs=[VMEM] * len(moved) + [VMEM, SMEM] + [VMEM] * 6,
        out_specs=VMEM,
        scratch_shapes=[
            pltpu.VMEM((length // LANES, devices * per, LANES), F32),
            pltpu.VMEM((length // LANES, devices * per, LANES), F32),
        ],
        name="long",
    )(*moved, spectrum, skip_gain, outer, outer_t, ahead, back, cos, sin)
    back_home = swap(long_out).reshape(channels, length)
    return (gate_long.astype(F32) * back_home.astype(F32)).astype(BF16)


def solution(mesh):
    placed = (
        P("ch", "ctx"),
        P("ch", "ctx"),
        P("ch", "ctx"),
        P("ch", "ctx"),
        P("ch", "ctx"),
        P("ch", None),
        P("ch", None),
        P(("ch", "ctx"), None),
        P("ch"),
    )
    return jax.shard_map(
        shards, mesh=mesh, in_specs=placed, out_specs=P("ch", "ctx"), check_vma=False
    )
```

```python
import jax
import jax.numpy as jnp
import numpy as np
from jax import lax
from jax.experimental import pallas as pl
from jax.experimental.pallas import tpu as pltpu
from jax.sharding import PartitionSpec as P

SPLIT = False
LANES = 128
VMEM = pl.BlockSpec(memory_space=pltpu.VMEM)
SMEM = pl.BlockSpec(memory_space=pltpu.SMEM)
BF16 = jnp.bfloat16
F32 = jnp.float32


def near_core(data):
    return pltpu.with_memory_space_constraint(data, pltpu.VMEM)


def in_hbm(data):
    return pltpu.with_memory_space_constraint(data, pltpu.HBM)


def call(kernel, outs, name, *args, specs=None, scratch=()):
    return pl.pallas_call(
        kernel,
        out_shape=outs,
        grid=(1,),
        in_specs=specs or [VMEM] * len(args),
        out_specs=(VMEM,) * len(outs) if isinstance(outs, tuple) else VMEM,
        scratch_shapes=list(scratch),
        compiler_params=pltpu.CompilerParams(vmem_limit_bytes=16 << 20),
        name=name,
    )(*args)


def matmul(a, b):
    return jnp.dot(a, b, preferred_element_type=F32)


def band(taps_ref, group):
    taps = taps_ref[pl.ds(group, 1), :].astype(F32)
    ring = jnp.concatenate([taps, jnp.zeros_like(taps)], axis=1)
    rows = jnp.broadcast_to(ring, (8, 2 * LANES))
    rows = pltpu.roll(rows, LANES, 1, stride=1, stride_axis=0)
    strips = [rows if m == 0 else pltpu.roll(rows, 8 * m, 1) for m in range(LANES // 8)]
    top = jnp.concatenate([s[:, :LANES] for s in strips], axis=0)
    bottom = jnp.concatenate([s[:, LANES:] for s in strips], axis=0)
    return jnp.concatenate([top, bottom], axis=0).astype(BF16)


def conv_blocks(wide, matrix, first, last):
    rows = wide.shape[0]
    stack = jnp.concatenate(
        [wide[:, b * LANES : (b + 2) * LANES] for b in range(first, last)], axis=0
    )
    out = matmul(stack, matrix)
    return jnp.concatenate([out[i * rows : (i + 1) * rows] for i in range(last - first)], axis=1)


def tail_kernel(value, key, gate_one, gate_two, taps, tails, matrices, mixed, one, two):
    groups = taps.shape[0]
    rows = value.shape[0] // groups
    width = mixed.shape[1]
    for g in range(groups):
        at = pl.ds(g * rows, rows)
        matrix = band(taps, g)
        matrices[g] = matrix
        block = (key[at, :].astype(F32) * value[at, :].astype(F32)).astype(BF16)
        tails[at, :LANES] = block[:, width:]
        first = conv_blocks(block[:, width - LANES :], matrix, 0, 1)
        tails[at, LANES:] = (gate_one[at, width:].astype(F32) * first).astype(BF16)
        mixed[at, :] = block[:, :width]
    one[...] = gate_one[:, :width]
    two[...] = gate_two[...]


def near_kernel(mixed, gate_one, gate_two, ahead, taps, tails, kept, out, matrices):
    groups = taps.shape[0]
    rows = mixed.shape[0] // groups
    for g in range(groups):
        at = pl.ds(g * rows, rows)
        matrix = band(taps, g)
        matrices[g] = matrix
        first = conv_blocks(mixed[at, :], ahead[g], 0, 2)
        first = (gate_one[at, LANES:].astype(F32) * first).astype(BF16)
        kept[at, :] = first[:, :LANES]
        first = jnp.concatenate([first, tails[at, LANES:]], axis=1)
        second = conv_blocks(first, matrix, 0, 2)
        out[at, :] = (gate_two[at, 2 * LANES :].astype(F32) * second).astype(BF16)


def edge_kernel(mixed, gate_one, gate_two, kept, matrices_one, matrices_two, halo, *refs):
    out = refs[-1]
    groups = matrices_one.shape[0]
    rows = mixed.shape[0] // groups
    for g in range(groups):
        at = pl.ds(g * rows, rows)
        first = jnp.concatenate([halo[at, :LANES], mixed[at, :LANES]], axis=1)
        first = conv_blocks(first, matrices_one[g], 0, 1)
        first = (gate_one[at, :LANES].astype(F32) * first).astype(BF16)
        first = jnp.concatenate([halo[at, LANES:], first, kept[at, :]], axis=1)
        second = conv_blocks(first, matrices_two[g], 0, 2)
        out[at, : 2 * LANES] = (gate_two[at, : 2 * LANES].astype(F32) * second).astype(BF16)
        if not SPLIT:
            out[at, 2 * LANES :] = refs[0][at, :]


def tables(length, devices):
    n = LANES
    per = length // n // devices
    order = np.arange(n)
    n1 = (order % devices) * per + order // devices
    k1 = np.arange(n) + 0.25
    outer = 2 * np.pi * np.outer(k1, n1) / n
    outer_table = np.concatenate([np.cos(outer), -np.sin(outer)], axis=0)
    inner = 2 * np.pi * np.outer(np.arange(n), np.arange(n)) / n
    cos, sin = np.cos(inner), np.sin(inner)
    ahead = np.block([[cos, -sin], [sin, cos]])
    back = np.block([[cos, sin], [-sin, cos]])
    turn = 2 * np.pi * np.outer(k1, np.arange(n)) / length
    half = lambda t: jnp.asarray(t, F32).astype(BF16)
    return (
        half(outer_table),
        half(outer_table.T),
        half(ahead),
        half(back),
        jnp.asarray(np.cos(turn), F32),
        jnp.asarray(np.sin(turn), F32),
    )


def gather_rows(rows, channel, channels):
    count = rows.shape[1] // channels
    picked = [rows[q, pl.ds(channel, count, stride=channels), :] for q in range(rows.shape[0])]
    return jnp.concatenate(picked, axis=0)


def transform(signals, outer, ahead, cos, sin):
    n = LANES
    parts = matmul(outer, jnp.concatenate([s.astype(BF16) for s in signals], axis=1))
    turned = []
    for c in range(len(signals)):
        re, im = parts[:n, c * n : (c + 1) * n], parts[n:, c * n : (c + 1) * n]
        both = jnp.concatenate([re * cos + im * sin, im * cos - re * sin], axis=1)
        turned.append(both.astype(BF16))
    return matmul(jnp.concatenate(turned, axis=0), ahead)


def filter_kernel(taps, outer, ahead, cos, sin, spectrum, rows):
    channels, length = taps.shape
    n = LANES
    per = rows.shape[0]
    for b in range(length // n):
        at = pl.ds(b // per * channels, channels)
        rows[b % per, at, :] = taps[:, b * n : (b + 1) * n].astype(F32)
    signals = [gather_rows(rows, c, channels) for c in range(channels)]
    waves = transform(signals, outer[...], ahead[...], cos[...], sin[...])
    spectrum[...] = (waves * (1.0 / length)).reshape(spectrum.shape)


def long_kernel(*refs):
    if SPLIT:
        late, early, spectrum, skip, outer, outer_t, ahead, back, cos, sin, out, rows, outs = refs
    else:
        early, spectrum, skip, outer, outer_t, ahead, back, cos, sin, out, rows, outs = refs
    n = LANES
    devices, channels, length = out.shape
    for part, piece in enumerate((early, late) if SPLIT else (early,)):
        width = piece.shape[2]
        flat = piece[...].astype(F32).reshape(devices * channels, width)
        for q in range(width // n):
            rows[part * (width // n) + q] = flat[:, q * n : (q + 1) * n]
    base = lax.axis_index("ctx") * channels
    cosines, sines = cos[...], sin[...]
    signals = [gather_rows(rows, c, channels) for c in range(channels)]
    waves = transform(signals, outer[...], ahead[...], cosines, sines)
    products = []
    for c in range(channels):
        re, im = waves[c * n : (c + 1) * n, :n], waves[c * n : (c + 1) * n, n:]
        filter_re, filter_im = spectrum[c, :, :n], spectrum[c, :, n:]
        both = [re * filter_re - im * filter_im, re * filter_im + im * filter_re]
        products.append(jnp.concatenate(both, axis=1).astype(BF16))
    waves = matmul(jnp.concatenate(products, axis=0), back[...])
    turned = []
    for c in range(channels):
        re, im = waves[c * n : (c + 1) * n, :n], waves[c * n : (c + 1) * n, n:]
        both = [re * cosines - im * sines, re * sines + im * cosines]
        turned.append(jnp.concatenate(both, axis=0).astype(BF16))
    results = matmul(outer_t[...], jnp.concatenate(turned, axis=1))
    for c in range(channels):
        result = results[:, c * n : (c + 1) * n] + skip[base + c] * signals[c]
        for q in range(length // n):
            at = pl.ds(c, devices, stride=channels)
            outs[q, at, :] = result[q * devices : (q + 1) * devices]
    for q in range(length // n):
        block = outs[q].reshape(devices, channels, n)
        out[:, :, q * n : (q + 1) * n] = block.astype(BF16)


def shards(
    value_in,
    key_in,
    gate_first,
    gate_second,
    gate_long,
    filter_first,
    filter_second,
    long_filter,
    skip_gain,
):
    channels, length = value_in.shape
    devices = lax.axis_size("ctx")
    per = channels // devices
    groups = filter_first.shape[0]
    half = length // 2
    outer, outer_t, ahead, back, cos, sin = [near_core(t) for t in tables(length * devices, devices)]
    bands = pltpu.VMEM((groups, 2 * LANES, LANES), BF16)
    width = length - LANES
    tails, ones, mixed, gate_one, gate_two = call(
        tail_kernel,
        (
            pltpu.VMEM((channels, 2 * LANES), BF16),
            bands,
            pltpu.VMEM((channels, width), BF16),
            pltpu.VMEM((channels, width), BF16),
            pltpu.VMEM((channels, length), BF16),
        ),
        "tail",
        *map(in_hbm, (value_in, key_in, gate_first, gate_second, filter_first)),
    )
    halo = lax.ppermute(tails, "ctx", [(i, i + 1) for i in range(devices - 1)])
    mixed, gate_one, gate_two, ones = map(near_core, (mixed, gate_one, gate_two, ones))
    kept, late, twos = call(
        near_kernel,
        (
            pltpu.VMEM((channels, LANES), BF16),
            pltpu.VMEM((channels, half), BF16),
            bands,
        ),
        "near",
        mixed,
        gate_one,
        gate_two,
        ones,
        near_core(filter_second),
        near_core(tails),
    )
    width = half if SPLIT else length
    rest = () if SPLIT else (near_core(late),)
    early = call(
        edge_kernel,
        pltpu.VMEM((channels, width), BF16),
        "edge",
        mixed,
        gate_one,
        gate_two,
        near_core(kept),
        ones,
        near_core(twos),
        near_core(halo),
        *rest,
    )
    plane = pltpu.VMEM((length // LANES, devices * per, LANES), F32)
    spectrum = call(
        filter_kernel,
        pltpu.VMEM((per, LANES, 2 * LANES), F32),
        "spectrum",
        near_core(long_filter),
        outer,
        ahead,
        cos,
        sin,
        scratch=[plane],
    )

    def swap(data):
        return lax.all_to_all(data, "ctx", split_axis=0, concat_axis=0, tiled=True)

    moved = [swap(early.reshape(devices, per, width))]
    if SPLIT:
        moved = [swap(late.reshape(devices, per, half))] + moved
    long_out = call(
        long_kernel,
        pltpu.VMEM((devices, per, length), BF16),
        "long",
        *map(near_core, moved),
        near_core(spectrum),
        skip_gain,
        outer,
        outer_t,
        ahead,
        back,
        cos,
        sin,
        specs=[VMEM] * (len(moved) + 1) + [SMEM] + [VMEM] * 6,
        scratch=[plane, plane],
    )
    back_home = swap(long_out).reshape(channels, length)
    return (gate_long.astype(F32) * back_home.astype(F32)).astype(BF16)


def solution(mesh):
    placed = (
        P("ch", "ctx"),
        P("ch", "ctx"),
        P("ch", "ctx"),
        P("ch", "ctx"),
        P("ch", "ctx"),
        P("ch", None),
        P("ch", None),
        P(("ch", "ctx"), None),
        P("ch"),
    )
    return jax.shard_map(
        shards, mesh=mesh, in_specs=placed, out_specs=P("ch", "ctx"), check_vma=False
    )
```

```python
import jax
import jax.numpy as jnp
import numpy as np
from jax import lax
from jax.experimental import pallas as pl
from jax.experimental.pallas import tpu as pltpu
from jax.sharding import PartitionSpec as P

SPLIT = False
LANES = 128
VMEM = pl.BlockSpec(memory_space=pltpu.VMEM)
SMEM = pl.BlockSpec(memory_space=pltpu.SMEM)
BF16 = jnp.bfloat16
F32 = jnp.float32


def near_core(data):
    return pltpu.with_memory_space_constraint(data, pltpu.VMEM)


def in_hbm(data):
    return pltpu.with_memory_space_constraint(data, pltpu.HBM)


def call(kernel, outs, name, *args, specs=None, scratch=()):
    return pl.pallas_call(
        kernel,
        out_shape=outs,
        grid=(1,),
        in_specs=specs or [VMEM] * len(args),
        out_specs=(VMEM,) * len(outs) if isinstance(outs, tuple) else VMEM,
        scratch_shapes=list(scratch),
        compiler_params=pltpu.CompilerParams(vmem_limit_bytes=16 << 20),
        name=name,
    )(*args)


def matmul(a, b):
    return jnp.dot(a, b, preferred_element_type=F32)


def band(taps_ref, group):
    taps = taps_ref[pl.ds(group, 1), :].astype(F32)
    ring = jnp.concatenate([taps, jnp.zeros_like(taps)], axis=1)
    rows = jnp.broadcast_to(ring, (8, 2 * LANES))
    rows = pltpu.roll(rows, LANES, 1, stride=1, stride_axis=0)
    strips = [rows if m == 0 else pltpu.roll(rows, 8 * m, 1) for m in range(LANES // 8)]
    top = jnp.concatenate([s[:, :LANES] for s in strips], axis=0)
    bottom = jnp.concatenate([s[:, LANES:] for s in strips], axis=0)
    return jnp.concatenate([top, bottom], axis=0).astype(BF16)


def conv_blocks(wide, matrix, first, last):
    rows = wide.shape[0]
    stack = jnp.concatenate(
        [wide[:, b * LANES : (b + 2) * LANES] for b in range(first, last)], axis=0
    )
    out = matmul(stack, matrix)
    return jnp.concatenate([out[i * rows : (i + 1) * rows] for i in range(last - first)], axis=1)


def tail_kernel(value, key, gate, taps, tails, matrices):
    groups = taps.shape[0]
    rows = value.shape[0] // groups
    for g in range(groups):
        at = pl.ds(g * rows, rows)
        matrix = band(taps, g)
        matrices[g] = matrix
        mixed = (key[at, :].astype(F32) * value[at, :].astype(F32)).astype(BF16)
        tails[at, :LANES] = mixed[:, LANES:]
        first = conv_blocks(mixed, matrix, 0, 1)
        tails[at, LANES:] = (gate[at, :].astype(F32) * first).astype(BF16)


def near_kernel(
    value, key, gate_one, gate_two, ahead, taps, tails, kept, out, matrices, mixed, one, two
):
    groups = taps.shape[0]
    rows = value.shape[0] // groups
    half = 2 * LANES
    for g in range(groups):
        at = pl.ds(g * rows, rows)
        matrix = band(taps, g)
        matrices[g] = matrix
        block = key[at, : 3 * LANES].astype(F32) * value[at, : 3 * LANES].astype(F32)
        block = block.astype(BF16)
        mixed[at, :] = block[:, :LANES]
        first = conv_blocks(block, ahead[g], 0, 2)
        first = (gate_one[at, LANES : 3 * LANES].astype(F32) * first).astype(BF16)
        kept[at, :] = first[:, :LANES]
        first = jnp.concatenate([first, tails[at, LANES:]], axis=1)
        second = conv_blocks(first, matrix, 0, 2)
        out[at, :] = (gate_two[at, half:].astype(F32) * second).astype(BF16)
    one[...] = gate_one[:, :LANES]
    two[...] = gate_two[:, :half]


def edge_kernel(mixed, gate_one, gate_two, kept, matrices_one, matrices_two, halo, *refs):
    out = refs[-1]
    groups = matrices_one.shape[0]
    rows = mixed.shape[0] // groups
    for g in range(groups):
        at = pl.ds(g * rows, rows)
        first = jnp.concatenate([halo[at, :LANES], mixed[at, :]], axis=1)
        first = conv_blocks(first, matrices_one[g], 0, 1)
        first = (gate_one[at, :].astype(F32) * first).astype(BF16)
        first = jnp.concatenate([halo[at, LANES:], first, kept[at, :]], axis=1)
        second = conv_blocks(first, matrices_two[g], 0, 2)
        out[at, : 2 * LANES] = (gate_two[at, :].astype(F32) * second).astype(BF16)
        if not SPLIT:
            out[at, 2 * LANES :] = refs[0][at, :]


def tables(length, devices):
    n = LANES
    per = length // n // devices
    order = np.arange(n)
    n1 = (order % devices) * per + order // devices
    k1 = np.arange(n) + 0.25
    outer = 2 * np.pi * np.outer(k1, n1) / n
    outer_table = np.concatenate([np.cos(outer), -np.sin(outer)], axis=0)
    inner = 2 * np.pi * np.outer(np.arange(n), np.arange(n)) / n
    cos, sin = np.cos(inner), np.sin(inner)
    ahead = np.block([[cos, -sin], [sin, cos]])
    back = np.block([[cos, sin], [-sin, cos]])
    turn = 2 * np.pi * np.outer(k1, np.arange(n)) / length
    half = lambda t: jnp.asarray(t, F32).astype(BF16)
    return (
        half(outer_table),
        half(outer_table.T),
        half(ahead),
        half(back),
        jnp.asarray(np.cos(turn), F32),
        jnp.asarray(np.sin(turn), F32),
    )


def gather_rows(rows, channel, channels):
    count = rows.shape[1] // channels
    picked = [rows[q, pl.ds(channel, count, stride=channels), :] for q in range(rows.shape[0])]
    return jnp.concatenate(picked, axis=0)


def transform(signals, outer, ahead, cos, sin):
    n = LANES
    parts = matmul(outer, jnp.concatenate([s.astype(BF16) for s in signals], axis=1))
    turned = []
    for c in range(len(signals)):
        re, im = parts[:n, c * n : (c + 1) * n], parts[n:, c * n : (c + 1) * n]
        both = jnp.concatenate([re * cos + im * sin, im * cos - re * sin], axis=1)
        turned.append(both.astype(BF16))
    return matmul(jnp.concatenate(turned, axis=0), ahead)


def filter_kernel(taps, outer, ahead, cos, sin, spectrum, rows):
    channels, length = taps.shape
    n = LANES
    per = rows.shape[0]
    for b in range(length // n):
        at = pl.ds(b // per * channels, channels)
        rows[b % per, at, :] = taps[:, b * n : (b + 1) * n].astype(F32)
    signals = [gather_rows(rows, c, channels) for c in range(channels)]
    waves = transform(signals, outer[...], ahead[...], cos[...], sin[...])
    spectrum[...] = (waves * (1.0 / length)).reshape(spectrum.shape)


def long_kernel(*refs):
    if SPLIT:
        late, early, spectrum, skip, outer, outer_t, ahead, back, cos, sin, out, rows, outs = refs
    else:
        early, spectrum, skip, outer, outer_t, ahead, back, cos, sin, out, rows, outs = refs
    n = LANES
    devices, channels, length = out.shape
    for part, piece in enumerate((early, late) if SPLIT else (early,)):
        width = piece.shape[2]
        flat = piece[...].astype(F32).reshape(devices * channels, width)
        for q in range(width // n):
            rows[part * (width // n) + q] = flat[:, q * n : (q + 1) * n]
    base = lax.axis_index("ctx") * channels
    cosines, sines = cos[...], sin[...]
    signals = [gather_rows(rows, c, channels) for c in range(channels)]
    waves = transform(signals, outer[...], ahead[...], cosines, sines)
    products = []
    for c in range(channels):
        re, im = waves[c * n : (c + 1) * n, :n], waves[c * n : (c + 1) * n, n:]
        filter_re, filter_im = spectrum[c, :, :n], spectrum[c, :, n:]
        both = [re * filter_re - im * filter_im, re * filter_im + im * filter_re]
        products.append(jnp.concatenate(both, axis=1).astype(BF16))
    waves = matmul(jnp.concatenate(products, axis=0), back[...])
    turned = []
    for c in range(channels):
        re, im = waves[c * n : (c + 1) * n, :n], waves[c * n : (c + 1) * n, n:]
        both = [re * cosines - im * sines, re * sines + im * cosines]
        turned.append(jnp.concatenate(both, axis=0).astype(BF16))
    results = matmul(outer_t[...], jnp.concatenate(turned, axis=1))
    for c in range(channels):
        result = results[:, c * n : (c + 1) * n] + skip[base + c] * signals[c]
        for q in range(length // n):
            at = pl.ds(c, devices, stride=channels)
            outs[q, at, :] = result[q * devices : (q + 1) * devices]
    for q in range(length // n):
        block = outs[q].reshape(devices, channels, n)
        out[:, :, q * n : (q + 1) * n] = block.astype(BF16)


def shards(
    value_in,
    key_in,
    gate_first,
    gate_second,
    gate_long,
    filter_first,
    filter_second,
    long_filter,
    skip_gain,
):
    channels, length = value_in.shape
    devices = lax.axis_size("ctx")
    per = channels // devices
    groups = filter_first.shape[0]
    half = length // 2
    outer, outer_t, ahead, back, cos, sin = [near_core(t) for t in tables(length * devices, devices)]
    bands = pltpu.VMEM((groups, 2 * LANES, LANES), BF16)
    block = pltpu.VMEM((channels, LANES), BF16)
    pair = pltpu.VMEM((channels, 2 * LANES), BF16)
    value, key, gate_one, gate_two = map(in_hbm, (value_in, key_in, gate_first, gate_second))
    tails, ones = call(
        tail_kernel,
        (pair, bands),
        "tail",
        value,
        key,
        gate_one,
        in_hbm(filter_first),
        specs=[
            pl.BlockSpec((channels, half), lambda i: (0, 1)),
            pl.BlockSpec((channels, half), lambda i: (0, 1)),
            pl.BlockSpec((channels, LANES), lambda i: (0, length // LANES - 1)),
            VMEM,
        ],
    )
    halo = lax.ppermute(tails, "ctx", [(i, i + 1) for i in range(devices - 1)])
    ones = near_core(ones)
    kept, late, twos, mixed, gate_one, gate_two = call(
        near_kernel,
        (block, pair, bands, block, block, pair),
        "near",
        value,
        key,
        gate_one,
        gate_two,
        ones,
        in_hbm(filter_second),
        near_core(tails),
    )
    plane = pltpu.VMEM((length // LANES, devices * per, LANES), F32)
    spectrum = call(
        filter_kernel,
        pltpu.VMEM((per, LANES, 2 * LANES), F32),
        "spectrum",
        near_core(long_filter),
        outer,
        ahead,
        cos,
        sin,
        scratch=[plane],
    )
    kept, spectrum = lax.optimization_barrier((kept, spectrum))
    mixed, gate_one, gate_two = map(near_core, (mixed, gate_one, gate_two))
    width = half if SPLIT else length
    rest = () if SPLIT else (near_core(late),)
    early = call(
        edge_kernel,
        pltpu.VMEM((channels, width), BF16),
        "edge",
        mixed,
        gate_one,
        gate_two,
        near_core(kept),
        ones,
        near_core(twos),
        near_core(halo),
        *rest,
    )

    def swap(data):
        return lax.all_to_all(data, "ctx", split_axis=0, concat_axis=0, tiled=True)

    moved = [swap(early.reshape(devices, per, width))]
    if SPLIT:
        moved = [swap(late.reshape(devices, per, half))] + moved
    long_out = call(
        long_kernel,
        pltpu.VMEM((devices, per, length), BF16),
        "long",
        *map(near_core, moved),
        near_core(spectrum),
        skip_gain,
        outer,
        outer_t,
        ahead,
        back,
        cos,
        sin,
        specs=[VMEM] * (len(moved) + 1) + [SMEM] + [VMEM] * 6,
        scratch=[plane, plane],
    )
    back_home = swap(long_out).reshape(channels, length)
    return (gate_long.astype(F32) * back_home.astype(F32)).astype(BF16)


def solution(mesh):
    placed = (
        P("ch", "ctx"),
        P("ch", "ctx"),
        P("ch", "ctx"),
        P("ch", "ctx"),
        P("ch", "ctx"),
        P("ch", None),
        P("ch", None),
        P(("ch", "ctx"), None),
        P("ch"),
    )
    return jax.shard_map(
        shards, mesh=mesh, in_specs=placed, out_specs=P("ch", "ctx"), check_vma=False
    )
```

```python
import jax
import jax.numpy as jnp
import numpy as np
from jax import lax
from jax.experimental import pallas as pl
from jax.experimental.pallas import tpu as pltpu
from jax.sharding import PartitionSpec as P


SPLIT = False
LANES = 128
ROW = 8
PARTS = 4
VMEM = pl.BlockSpec(memory_space=pltpu.VMEM)
SMEM = pl.BlockSpec(memory_space=pltpu.SMEM)
BF16 = jnp.bfloat16
F32 = jnp.float32


def near_core(data):
    return pltpu.with_memory_space_constraint(data, pltpu.VMEM)


def in_hbm(data):
    return pltpu.with_memory_space_constraint(data, pltpu.HBM)


def call(kernel, outs, *args, specs=None, scratch=()):
    return pl.pallas_call(
        kernel,
        out_shape=outs,
        grid=(1,),
        in_specs=specs or [VMEM] * len(args),
        out_specs=(VMEM,) * len(outs) if isinstance(outs, tuple) else VMEM,
        scratch_shapes=list(scratch),
        compiler_params=pltpu.CompilerParams(vmem_limit_bytes=16 << 20),
    )(*args)


def matmul(a, b):
    return jnp.dot(a, b, preferred_element_type=F32)


def band(taps_ref, group):
    taps = taps_ref[pl.ds(group, 1), :].astype(F32)
    ring = jnp.concatenate([taps, jnp.zeros_like(taps)], axis=1)
    rows = jnp.broadcast_to(ring, (8, 2 * LANES))
    rows = pltpu.roll(rows, LANES, 1, stride=1, stride_axis=0)
    strips = [rows if m == 0 else pltpu.roll(rows, 8 * m, 1) for m in range(LANES // 8)]
    top = jnp.concatenate([s[:, :LANES] for s in strips], axis=0)
    bottom = jnp.concatenate([s[:, LANES:] for s in strips], axis=0)
    return jnp.concatenate([top, bottom], axis=0).astype(BF16)


def conv_blocks(wide, matrix, first, last):
    rows = wide.shape[0]
    stack = jnp.concatenate(
        [wide[:, b * LANES : (b + 2) * LANES] for b in range(first, last)], axis=0
    )
    out = matmul(stack, matrix)
    return jnp.concatenate([out[i * rows : (i + 1) * rows] for i in range(last - first)], axis=1)


def tail_kernel(value, key, gate, taps, tails, matrices):
    groups = taps.shape[0]
    rows = value.shape[0] // groups
    for g in range(groups):
        at = pl.ds(g * rows, rows)
        matrix = band(taps, g)
        matrices[g] = matrix
        mixed = (key[at, :].astype(F32) * value[at, :].astype(F32)).astype(BF16)
        tails[at, :LANES] = mixed[:, LANES:]
        first = conv_blocks(mixed, matrix, 0, 1)
        tails[at, LANES:] = (gate[at, :].astype(F32) * first).astype(BF16)


def near_kernel(
    value, key, gate_one, gate_two, ahead, taps, tails, kept, out, matrices, mixed, one, two
):
    groups = taps.shape[0]
    rows = value.shape[0] // groups
    half = 2 * LANES
    for g in range(groups):
        at = pl.ds(g * rows, rows)
        matrix = band(taps, g)
        matrices[g] = matrix
        block = key[at, : 3 * LANES].astype(F32) * value[at, : 3 * LANES].astype(F32)
        block = block.astype(BF16)
        mixed[at, :] = block[:, :LANES]
        first = conv_blocks(block, ahead[g], 0, 2)
        first = (gate_one[at, LANES : 3 * LANES].astype(F32) * first).astype(BF16)
        kept[at, :] = first[:, :LANES]
        first = jnp.concatenate([first, tails[at, LANES:]], axis=1)
        second = conv_blocks(first, matrix, 0, 2)
        out[at, :] = (gate_two[at, half:].astype(F32) * second).astype(BF16)
    one[...] = gate_one[:, :LANES]
    two[...] = gate_two[:, :half]


def edge_kernel(mixed, gate_one, gate_two, kept, matrices_one, matrices_two, far, close, *refs):
    out = refs[-1]
    groups = matrices_one.shape[0]
    rows = mixed.shape[0] // groups
    for g in range(groups):
        at = pl.ds(g * rows, rows)
        halo = far[at, :] + close[at, :]
        first = jnp.concatenate([halo[:, :LANES], mixed[at, :]], axis=1)
        first = conv_blocks(first, matrices_one[g], 0, 1)
        first = (gate_one[at, :].astype(F32) * first).astype(BF16)
        first = jnp.concatenate([halo[:, LANES:], first, kept[at, :]], axis=1)
        second = conv_blocks(first, matrices_two[g], 0, 2)
        out[at, : 2 * LANES] = (gate_two[at, :].astype(F32) * second).astype(BF16)
        if not SPLIT:
            out[at, 2 * LANES :] = refs[0][at, :]


def tables(length, devices):
    n = LANES
    per = length // n // devices
    order = np.arange(n)
    n1 = (order % devices) * per + order // devices
    k1 = np.arange(n) + 0.25
    outer = 2 * np.pi * np.outer(k1, n1) / n
    outer_table = np.concatenate([np.cos(outer), -np.sin(outer)], axis=0)
    inner = 2 * np.pi * np.outer(np.arange(n), np.arange(n)) / n
    cos, sin = np.cos(inner), np.sin(inner)
    ahead = np.block([[cos, -sin], [sin, cos]])
    back = np.block([[cos, sin], [-sin, cos]])
    turn = 2 * np.pi * np.outer(k1, np.arange(n)) / length
    half = lambda t: jnp.asarray(t, F32).astype(BF16)
    return (
        half(outer_table),
        half(outer_table.T),
        half(ahead),
        half(back),
        jnp.asarray(np.cos(turn), F32),
        jnp.asarray(np.sin(turn), F32),
    )


def gather_rows(rows, channel, channels):
    count = rows.shape[1] // channels
    picked = [rows[q, pl.ds(channel, count, stride=channels), :] for q in range(rows.shape[0])]
    return jnp.concatenate(picked, axis=0)


def transform(signals, outer, ahead, cos, sin):
    n = LANES
    parts = matmul(outer, jnp.concatenate([s.astype(BF16) for s in signals], axis=1))
    turned = []
    for c in range(len(signals)):
        re, im = parts[:n, c * n : (c + 1) * n], parts[n:, c * n : (c + 1) * n]
        both = jnp.concatenate([re * cos + im * sin, im * cos - re * sin], axis=1)
        turned.append(both.astype(BF16))
    return matmul(jnp.concatenate(turned, axis=0), ahead)


def filter_kernel(taps, outer, ahead, cos, sin, spectrum, rows):
    channels, length = taps.shape
    n = LANES
    per = rows.shape[0]
    for b in range(length // n):
        at = pl.ds(b // per * channels, channels)
        rows[b % per, at, :] = taps[:, b * n : (b + 1) * n].astype(F32)
    signals = [gather_rows(rows, c, channels) for c in range(channels)]
    waves = transform(signals, outer[...], ahead[...], cos[...], sin[...])
    spectrum[...] = (waves * (1.0 / length)).reshape(spectrum.shape)


def long_kernel(*refs):
    if SPLIT:
        late, early, spectrum, skip, outer, outer_t, ahead, back, cos, sin, out, rows, outs = refs
    else:
        early, spectrum, skip, outer, outer_t, ahead, back, cos, sin, out, rows, outs = refs
    n = LANES
    devices, channels, length = out.shape
    for part, piece in enumerate((early, late) if SPLIT else (early,)):
        width = piece.shape[2]
        flat = piece[...].astype(F32).reshape(devices * channels, width)
        for q in range(width // n):
            rows[part * (width // n) + q] = flat[:, q * n : (q + 1) * n]
    base = lax.axis_index("ctx") * channels
    cosines, sines = cos[...], sin[...]
    signals = [gather_rows(rows, c, channels) for c in range(channels)]
    waves = transform(signals, outer[...], ahead[...], cosines, sines)
    products = []
    for c in range(channels):
        re, im = waves[c * n : (c + 1) * n, :n], waves[c * n : (c + 1) * n, n:]
        filter_re, filter_im = spectrum[c, :, :n], spectrum[c, :, n:]
        both = [re * filter_re - im * filter_im, re * filter_im + im * filter_re]
        products.append(jnp.concatenate(both, axis=1).astype(BF16))
    waves = matmul(jnp.concatenate(products, axis=0), back[...])
    turned = []
    for c in range(channels):
        re, im = waves[c * n : (c + 1) * n, :n], waves[c * n : (c + 1) * n, n:]
        both = [re * cosines - im * sines, re * sines + im * cosines]
        turned.append(jnp.concatenate(both, axis=0).astype(BF16))
    results = matmul(outer_t[...], jnp.concatenate(turned, axis=1))
    for c in range(channels):
        result = results[:, c * n : (c + 1) * n] + skip[base + c] * signals[c]
        for q in range(length // n):
            at = pl.ds(c, devices, stride=channels)
            outs[q, at, :] = result[q * devices : (q + 1) * devices]
    for q in range(length // n):
        block = outs[q].reshape(devices, channels, n)
        out[:, :, q * n : (q + 1) * n] = block.astype(BF16)


def gate_kernel(gate, data, out, held, sems):
    rows = gate.shape[0] // PARTS
    copies = []
    for p in range(PARTS):
        at = pl.ds(p * rows, rows)
        held[p] = (gate[at, :].astype(F32) * data[at, :].astype(F32)).astype(BF16)
        copies.append(pltpu.make_async_copy(held.at[p], out.at[at, :], sems.at[p]))
        copies[-1].start()
    for copy in copies:
        copy.wait()


def shards(
    value_in,
    key_in,
    gate_first,
    gate_second,
    gate_long,
    filter_first,
    filter_second,
    long_filter,
    skip_gain,
):
    channels, length = value_in.shape
    devices = lax.axis_size("ctx")
    per = channels // devices
    groups = filter_first.shape[0]
    half = length // 2
    outer, outer_t, ahead, back, cos, sin = [near_core(t) for t in tables(length * devices, devices)]
    bands = pltpu.VMEM((groups, 2 * LANES, LANES), BF16)
    block = pltpu.VMEM((channels, LANES), BF16)
    pair = pltpu.VMEM((channels, 2 * LANES), BF16)
    value, key, gate_one, gate_two = map(in_hbm, (value_in, key_in, gate_first, gate_second))
    tails, ones = call(
        tail_kernel,
        (pair, bands),
        value,
        key,
        gate_one,
        in_hbm(filter_first),
        specs=[
            pl.BlockSpec((channels, half), lambda i: (0, 1)),
            pl.BlockSpec((channels, half), lambda i: (0, 1)),
            pl.BlockSpec((channels, LANES), lambda i: (0, length // LANES - 1)),
            VMEM,
        ],
    )
    pairs = [(i, i + 1) for i in range(devices - 1)]
    far = lax.ppermute(tails, "ctx", [p for p in pairs if p[1] % ROW == 0])
    close = lax.ppermute(tails, "ctx", [p for p in pairs if p[1] % ROW])
    ones = near_core(ones)
    kept, late, twos, mixed, gate_one, gate_two = call(
        near_kernel,
        (block, pair, bands, block, block, pair),
        value,
        key,
        gate_one,
        gate_two,
        ones,
        in_hbm(filter_second),
        near_core(tails),
    )
    plane = pltpu.VMEM((length // LANES, devices * per, LANES), F32)
    spectrum = call(
        filter_kernel,
        pltpu.VMEM((per, LANES, 2 * LANES), F32),
        near_core(long_filter),
        outer,
        ahead,
        cos,
        sin,
        scratch=[plane],
    )
    kept, spectrum = lax.optimization_barrier((kept, spectrum))
    mixed, gate_one, gate_two = map(near_core, (mixed, gate_one, gate_two))
    width = half if SPLIT else length
    rest = () if SPLIT else (near_core(late),)
    early = call(
        edge_kernel,
        pltpu.VMEM((channels, width), BF16),
        mixed,
        gate_one,
        gate_two,
        near_core(kept),
        ones,
        near_core(twos),
        near_core(far),
        near_core(close),
        *rest,
    )

    def swap(data):
        return lax.all_to_all(data, "ctx", split_axis=0, concat_axis=0, tiled=True)

    moved = [swap(early.reshape(devices, per, width))]
    if SPLIT:
        moved = [swap(late.reshape(devices, per, half))] + moved
    long_out = call(
        long_kernel,
        pltpu.VMEM((devices, per, length), BF16),
        *map(near_core, moved),
        near_core(spectrum),
        skip_gain,
        outer,
        outer_t,
        ahead,
        back,
        cos,
        sin,
        specs=[VMEM] * (len(moved) + 1) + [SMEM] + [VMEM] * 6,
        scratch=[plane, plane],
    )
    back_home = swap(long_out).reshape(channels, length)
    return pl.pallas_call(
        gate_kernel,
        out_shape=jax.ShapeDtypeStruct((channels, length), BF16),
        in_specs=[VMEM, VMEM],
        out_specs=pl.BlockSpec(memory_space=pl.ANY),
        scratch_shapes=[
            pltpu.VMEM((PARTS, channels // PARTS, length), BF16),
            pltpu.SemaphoreType.DMA((PARTS,)),
        ],
        compiler_params=pltpu.CompilerParams(vmem_limit_bytes=16 << 20),
        name="gate",
    )(near_core(gate_long), near_core(back_home))


def solution(mesh):
    placed = (
        P("ch", "ctx"),
        P("ch", "ctx"),
        P("ch", "ctx"),
        P("ch", "ctx"),
        P("ch", "ctx"),
        P("ch", None),
        P("ch", None),
        P(("ch", "ctx"), None),
        P("ch"),
    )
    return jax.shard_map(
        shards, mesh=mesh, in_specs=placed, out_specs=P("ch", "ctx"), check_vma=False
    )
```

```python
import jax
import jax.numpy as jnp
import numpy as np
from jax import lax
from jax.experimental import pallas as pl
from jax.experimental.pallas import tpu as pltpu
from jax.sharding import PartitionSpec as P


SPLIT = False
LANES = 128
ROW = 8
PARTS = 4
BATCH = 2
VMEM = pl.BlockSpec(memory_space=pltpu.VMEM)
SMEM = pl.BlockSpec(memory_space=pltpu.SMEM)
BF16 = jnp.bfloat16
F32 = jnp.float32


def near_core(data):
    return pltpu.with_memory_space_constraint(data, pltpu.VMEM)


def in_hbm(data):
    return pltpu.with_memory_space_constraint(data, pltpu.HBM)


def call(kernel, outs, *args, specs=None, scratch=()):
    return pl.pallas_call(
        kernel,
        out_shape=outs,
        grid=(1,),
        in_specs=specs or [VMEM] * len(args),
        out_specs=(VMEM,) * len(outs) if isinstance(outs, tuple) else VMEM,
        scratch_shapes=list(scratch),
        compiler_params=pltpu.CompilerParams(vmem_limit_bytes=16 << 20),
    )(*args)


def matmul(a, b):
    return jnp.dot(a, b, preferred_element_type=F32)


def band(taps_ref, group):
    taps = taps_ref[pl.ds(group, 1), :].astype(F32)
    ring = jnp.concatenate([taps, jnp.zeros_like(taps)], axis=1)
    rows = jnp.broadcast_to(ring, (8, 2 * LANES))
    rows = pltpu.roll(rows, LANES, 1, stride=1, stride_axis=0)
    strips = [rows if m == 0 else pltpu.roll(rows, 8 * m, 1) for m in range(LANES // 8)]
    top = jnp.concatenate([s[:, :LANES] for s in strips], axis=0)
    bottom = jnp.concatenate([s[:, LANES:] for s in strips], axis=0)
    return jnp.concatenate([top, bottom], axis=0).astype(BF16)


def conv_blocks(wide, matrix, first, last):
    rows = wide.shape[0]
    stack = jnp.concatenate(
        [wide[:, b * LANES : (b + 2) * LANES] for b in range(first, last)], axis=0
    )
    out = matmul(stack, matrix)
    return jnp.concatenate([out[i * rows : (i + 1) * rows] for i in range(last - first)], axis=1)


def tail_kernel(value, key, gate, taps, tails, matrices, values, keys, gates, held, sems):
    groups = taps.shape[0]
    rows, length = value.shape[0] // groups, value.shape[1]
    width = values.shape[1]
    copies = [
        pltpu.make_async_copy(source, target, sems.at[i])
        for i, (source, target) in enumerate(
            (
                (taps, held),
                (value.at[:, pl.ds(length - width, width)], values),
                (key.at[:, pl.ds(length - width, width)], keys),
                (gate.at[:, pl.ds(length - LANES, LANES)], gates),
            )
        )
    ]
    for copy in copies:
        copy.start()
    copies[0].wait()
    for g in range(groups // 2):
        matrices[g] = band(held, g)
    for copy in copies[1:]:
        copy.wait()
    for g in range(groups):
        at = pl.ds(g * rows, rows)
        if g >= groups // 2:
            matrices[g] = band(held, g)
        mixed = (keys[at, :].astype(F32) * values[at, :].astype(F32)).astype(BF16)
        tails[at, :LANES] = mixed[:, LANES:]
        first = conv_blocks(mixed, matrices[g], 0, 1)
        tails[at, LANES:] = (gates[at, :].astype(F32) * first).astype(BF16)


def near_kernel(
    value, key, gate_one, gate_two, ahead, taps, tails, kept, out, matrices, mixed, one, two
):
    groups = taps.shape[0]
    rows = value.shape[0] // groups
    half = 2 * LANES
    for g in range(groups):
        at = pl.ds(g * rows, rows)
        matrix = band(taps, g)
        matrices[g] = matrix
        block = key[at, : 3 * LANES].astype(F32) * value[at, : 3 * LANES].astype(F32)
        block = block.astype(BF16)
        mixed[at, :] = block[:, :LANES]
        first = conv_blocks(block, ahead[g], 0, 2)
        first = (gate_one[at, LANES : 3 * LANES].astype(F32) * first).astype(BF16)
        kept[at, :] = first[:, :LANES]
        first = jnp.concatenate([first, tails[at, LANES:]], axis=1)
        second = conv_blocks(first, matrix, 0, 2)
        out[at, :] = (gate_two[at, half:].astype(F32) * second).astype(BF16)
    one[...] = gate_one[:, :LANES]
    two[...] = gate_two[:, :half]


def edge_kernel(mixed, gate_one, gate_two, kept, matrices_one, matrices_two, far, close, *refs):
    out = refs[-1]
    groups = matrices_one.shape[0]
    rows = mixed.shape[0] // groups
    for g in range(groups):
        at = pl.ds(g * rows, rows)
        halo = far[at, :] + close[at, :]
        first = jnp.concatenate([halo[:, :LANES], mixed[at, :]], axis=1)
        first = conv_blocks(first, matrices_one[g], 0, 1)
        first = (gate_one[at, :].astype(F32) * first).astype(BF16)
        first = jnp.concatenate([halo[:, LANES:], first, kept[at, :]], axis=1)
        second = conv_blocks(first, matrices_two[g], 0, 2)
        out[at, : 2 * LANES] = (gate_two[at, :].astype(F32) * second).astype(BF16)
        if not SPLIT:
            out[at, 2 * LANES :] = refs[0][at, :]


def tables(length, devices):
    n = LANES
    per = length // n // devices
    order = np.arange(n)
    n1 = (order % devices) * per + order // devices
    k1 = np.arange(n) + 0.25
    outer = 2 * np.pi * np.outer(k1, n1) / n
    outer_table = np.concatenate([np.cos(outer), -np.sin(outer)], axis=0)
    inner = 2 * np.pi * np.outer(np.arange(n), np.arange(n)) / n
    cos, sin = np.cos(inner), np.sin(inner)
    ahead = np.block([[cos, -sin], [sin, cos]])
    back = np.block([[cos, sin], [-sin, cos]])
    turn = 2 * np.pi * np.outer(k1, np.arange(n)) / length
    half = lambda t: jnp.asarray(t, F32).astype(BF16)
    return (
        half(outer_table),
        half(outer_table.T),
        half(ahead),
        half(back),
        jnp.asarray(np.cos(turn), F32),
        jnp.asarray(np.sin(turn), F32),
    )


def gather_rows(rows, channel, channels):
    count = rows.shape[1] // channels
    picked = [rows[q, pl.ds(channel, count, stride=channels), :] for q in range(rows.shape[0])]
    return jnp.concatenate(picked, axis=0)


def side_by_side(signals):
    return jnp.concatenate([s.astype(BF16) for s in signals], axis=1)


def turn_ahead(parts, cos, sin):
    n = LANES
    turned = []
    for at in range(0, parts.shape[1], n):
        re, im = parts[:n, at : at + n], parts[n:, at : at + n]
        both = jnp.concatenate([re * cos + im * sin, im * cos - re * sin], axis=1)
        turned.append(both.astype(BF16))
    return jnp.concatenate(turned, axis=0)


def weigh(waves, spectra):
    n = LANES
    products = []
    for i, spectrum in enumerate(spectra):
        re, im = waves[i * n : (i + 1) * n, :n], waves[i * n : (i + 1) * n, n:]
        filter_re, filter_im = spectrum[:, :n], spectrum[:, n:]
        both = [re * filter_re - im * filter_im, re * filter_im + im * filter_re]
        products.append(jnp.concatenate(both, axis=1).astype(BF16))
    return jnp.concatenate(products, axis=0)


def turn_back(waves, cos, sin):
    n = LANES
    turned = []
    for at in range(0, waves.shape[0], n):
        re, im = waves[at : at + n, :n], waves[at : at + n, n:]
        both = [re * cos - im * sin, re * sin + im * cos]
        turned.append(jnp.concatenate(both, axis=0).astype(BF16))
    return jnp.concatenate(turned, axis=1)


def filter_kernel(taps, outer, ahead, cos, sin, spectrum, rows):
    channels, length = taps.shape
    n = LANES
    per = rows.shape[0]
    for b in range(length // n):
        at = pl.ds(b // per * channels, channels)
        rows[b % per, at, :] = taps[:, b * n : (b + 1) * n].astype(F32)
    signals = [gather_rows(rows, c, channels) for c in range(channels)]
    waves = matmul(outer[...], side_by_side(signals))
    waves = matmul(turn_ahead(waves, cos[...], sin[...]), ahead[...])
    spectrum[...] = (waves * (1.0 / length)).reshape(spectrum.shape)


def long_kernel(*refs):
    if SPLIT:
        late, early, spectrum, skip, outer, outer_t, ahead, back, cos, sin, out, rows, outs = refs
    else:
        early, spectrum, skip, outer, outer_t, ahead, back, cos, sin, out, rows, outs = refs
    n = LANES
    devices, channels, length = out.shape
    for part, piece in enumerate((early, late) if SPLIT else (early,)):
        width = piece.shape[2]
        flat = piece[...].astype(F32).reshape(devices * channels, width)
        for q in range(width // n):
            rows[part * (width // n) + q] = flat[:, q * n : (q + 1) * n]
    base = lax.axis_index("ctx") * channels
    cosines, sines = cos[...], sin[...]
    batches = [range(c, c + BATCH) for c in range(0, channels, BATCH)]
    signals = [[gather_rows(rows, c, channels) for c in batch] for batch in batches]
    waves = [matmul(outer[...], side_by_side(s)) for s in signals]
    waves = [matmul(turn_ahead(w, cosines, sines), ahead[...]) for w in waves]
    waves = [
        matmul(weigh(w, [spectrum[c] for c in batch]), back[...])
        for w, batch in zip(waves, batches)
    ]
    waves = [matmul(outer_t[...], turn_back(w, cosines, sines)) for w in waves]
    for batch, signal, result in zip(batches, signals, waves):
        for i, c in enumerate(batch):
            block = result[:, i * n : (i + 1) * n] + skip[base + c] * signal[i]
            for q in range(length // n):
                at = pl.ds(c, devices, stride=channels)
                outs[q, at, :] = block[q * devices : (q + 1) * devices]
    for q in range(length // n):
        block = outs[q].reshape(devices, channels, n)
        out[:, :, q * n : (q + 1) * n] = block.astype(BF16)


def gate_kernel(gate, data, out, held, sems):
    rows = gate.shape[0] // PARTS
    copies = []
    for p in range(PARTS):
        at = pl.ds(p * rows, rows)
        held[p] = (gate[at, :].astype(F32) * data[at, :].astype(F32)).astype(BF16)
        copies.append(pltpu.make_async_copy(held.at[p], out.at[at, :], sems.at[p]))
        copies[-1].start()
    for copy in copies:
        copy.wait()


def shards(
    value_in,
    key_in,
    gate_first,
    gate_second,
    gate_long,
    filter_first,
    filter_second,
    long_filter,
    skip_gain,
):
    channels, length = value_in.shape
    devices = lax.axis_size("ctx")
    per = channels // devices
    groups = filter_first.shape[0]
    half = length // 2
    outer, outer_t, ahead, back, cos, sin = [near_core(t) for t in tables(length * devices, devices)]
    bands = pltpu.VMEM((groups, 2 * LANES, LANES), BF16)
    block = pltpu.VMEM((channels, LANES), BF16)
    pair = pltpu.VMEM((channels, 2 * LANES), BF16)
    value, key, gate_one, gate_two = map(in_hbm, (value_in, key_in, gate_first, gate_second))
    tails, ones = call(
        tail_kernel,
        (pair, bands),
        value,
        key,
        gate_one,
        in_hbm(filter_first),
        specs=[pl.BlockSpec(memory_space=pl.ANY)] * 4,
        scratch=[
            pair,
            pair,
            block,
            pltpu.VMEM(filter_first.shape, BF16),
            pltpu.SemaphoreType.DMA((4,)),
        ],
    )
    pairs = [(i, i + 1) for i in range(devices - 1)]
    far = lax.ppermute(tails, "ctx", [p for p in pairs if p[1] % ROW == 0])
    close = lax.ppermute(tails, "ctx", [p for p in pairs if p[1] % ROW])
    ones = near_core(ones)
    kept, late, twos, mixed, gate_one, gate_two = call(
        near_kernel,
        (block, pair, bands, block, block, pair),
        value,
        key,
        gate_one,
        gate_two,
        ones,
        in_hbm(filter_second),
        near_core(tails),
    )
    plane = pltpu.VMEM((length // LANES, devices * per, LANES), F32)
    spectrum = call(
        filter_kernel,
        pltpu.VMEM((per, LANES, 2 * LANES), F32),
        near_core(long_filter),
        outer,
        ahead,
        cos,
        sin,
        scratch=[plane],
    )
    kept, spectrum = lax.optimization_barrier((kept, spectrum))
    mixed, gate_one, gate_two = map(near_core, (mixed, gate_one, gate_two))
    width = half if SPLIT else length
    rest = () if SPLIT else (near_core(late),)
    early = call(
        edge_kernel,
        pltpu.VMEM((channels, width), BF16),
        mixed,
        gate_one,
        gate_two,
        near_core(kept),
        ones,
        near_core(twos),
        near_core(far),
        near_core(close),
        *rest,
    )

    def swap(data):
        return lax.all_to_all(data, "ctx", split_axis=0, concat_axis=0, tiled=True)

    moved = [swap(early.reshape(devices, per, width))]
    if SPLIT:
        moved = [swap(late.reshape(devices, per, half))] + moved
    long_out = call(
        long_kernel,
        pltpu.VMEM((devices, per, length), BF16),
        *map(near_core, moved),
        near_core(spectrum),
        skip_gain,
        outer,
        outer_t,
        ahead,
        back,
        cos,
        sin,
        specs=[VMEM] * (len(moved) + 1) + [SMEM] + [VMEM] * 6,
        scratch=[plane, plane],
    )
    back_home = swap(long_out).reshape(channels, length)
    return pl.pallas_call(
        gate_kernel,
        out_shape=jax.ShapeDtypeStruct((channels, length), BF16),
        in_specs=[VMEM, VMEM],
        out_specs=pl.BlockSpec(memory_space=pl.ANY),
        scratch_shapes=[
            pltpu.VMEM((PARTS, channels // PARTS, length), BF16),
            pltpu.SemaphoreType.DMA((PARTS,)),
        ],
        compiler_params=pltpu.CompilerParams(vmem_limit_bytes=16 << 20),
        name="gate",
    )(near_core(gate_long), near_core(back_home))


def solution(mesh):
    placed = (
        P("ch", "ctx"),
        P("ch", "ctx"),
        P("ch", "ctx"),
        P("ch", "ctx"),
        P("ch", "ctx"),
        P("ch", None),
        P("ch", None),
        P(("ch", "ctx"), None),
        P("ch"),
    )
    return jax.shard_map(
        shards, mesh=mesh, in_specs=placed, out_specs=P("ch", "ctx"), check_vma=False
    )
```

```python
import jax
import jax.numpy as jnp
import numpy as np
from jax import lax
from jax.experimental import pallas as pl
from jax.experimental.pallas import tpu as pltpu
from jax.sharding import PartitionSpec as P


SPLIT = False
LANES = 128
ROW = 8
PARTS = 2
BATCH = 1
VMEM = pl.BlockSpec(memory_space=pltpu.VMEM)
SMEM = pl.BlockSpec(memory_space=pltpu.SMEM)
BF16 = jnp.bfloat16
F32 = jnp.float32


def near_core(data):
    return pltpu.with_memory_space_constraint(data, pltpu.VMEM)


def in_hbm(data):
    return pltpu.with_memory_space_constraint(data, pltpu.HBM)


def call(kernel, outs, *args, specs=None, scratch=()):
    return pl.pallas_call(
        kernel,
        out_shape=outs,
        grid=(1,),
        in_specs=specs or [VMEM] * len(args),
        out_specs=(VMEM,) * len(outs) if isinstance(outs, tuple) else VMEM,
        scratch_shapes=list(scratch),
        compiler_params=pltpu.CompilerParams(vmem_limit_bytes=16 << 20),
    )(*args)


def matmul(a, b):
    return jnp.dot(a, b, preferred_element_type=F32)


def band(taps_ref, group):
    taps = taps_ref[pl.ds(group, 1), :].astype(F32)
    ring = jnp.concatenate([taps, jnp.zeros_like(taps)], axis=1)
    rows = jnp.broadcast_to(ring, (8, 2 * LANES))
    rows = pltpu.roll(rows, LANES, 1, stride=1, stride_axis=0)
    strips = [rows if m == 0 else pltpu.roll(rows, 8 * m, 1) for m in range(LANES // 8)]
    top = jnp.concatenate([s[:, :LANES] for s in strips], axis=0)
    bottom = jnp.concatenate([s[:, LANES:] for s in strips], axis=0)
    return jnp.concatenate([top, bottom], axis=0).astype(BF16)


def conv_blocks(wide, matrix, first, last):
    rows = wide.shape[0]
    stack = jnp.concatenate(
        [wide[:, b * LANES : (b + 2) * LANES] for b in range(first, last)], axis=0
    )
    out = matmul(stack, matrix)
    return jnp.concatenate([out[i * rows : (i + 1) * rows] for i in range(last - first)], axis=1)


def tail_kernel(value, key, gate, taps, tails, matrices, values, keys, gates, held, sems):
    groups = taps.shape[0]
    rows, length = value.shape[0] // groups, value.shape[1]
    width = values.shape[1]
    copies = [
        pltpu.make_async_copy(source, target, sems.at[i])
        for i, (source, target) in enumerate(
            (
                (taps, held),
                (value.at[:, pl.ds(length - width, width)], values),
                (key.at[:, pl.ds(length - width, width)], keys),
                (gate.at[:, pl.ds(length - LANES, LANES)], gates),
            )
        )
    ]
    for copy in copies:
        copy.start()
    copies[0].wait()
    for g in range(groups // 2):
        matrices[g] = band(held, g)
    for copy in copies[1:]:
        copy.wait()
    for g in range(groups):
        at = pl.ds(g * rows, rows)
        if g >= groups // 2:
            matrices[g] = band(held, g)
        mixed = (keys[at, :].astype(F32) * values[at, :].astype(F32)).astype(BF16)
        tails[at, :LANES] = mixed[:, LANES:]
        first = conv_blocks(mixed, matrices[g], 0, 1)
        tails[at, LANES:] = (gates[at, :].astype(F32) * first).astype(BF16)


def near_kernel(
    value, key, gate_one, gate_two, ahead, taps, tails, kept, out, matrices, mixed, one, two
):
    groups = taps.shape[0]
    rows = value.shape[0] // groups
    half = 2 * LANES
    for g in range(groups):
        at = pl.ds(g * rows, rows)
        matrix = band(taps, g)
        matrices[g] = matrix
        block = key[at, : 3 * LANES].astype(F32) * value[at, : 3 * LANES].astype(F32)
        block = block.astype(BF16)
        mixed[at, :] = block[:, :LANES]
        first = conv_blocks(block, ahead[g], 0, 2)
        first = (gate_one[at, LANES : 3 * LANES].astype(F32) * first).astype(BF16)
        kept[at, :] = first[:, :LANES]
        first = jnp.concatenate([first, tails[at, LANES:]], axis=1)
        second = conv_blocks(first, matrix, 0, 2)
        out[at, :] = (gate_two[at, half:].astype(F32) * second).astype(BF16)
    one[...] = gate_one[:, :LANES]
    two[...] = gate_two[:, :half]


def edge_kernel(mixed, gate_one, gate_two, kept, matrices_one, matrices_two, far, close, *refs):
    out = refs[-1]
    groups = matrices_one.shape[0]
    rows = mixed.shape[0] // groups
    places = [pl.ds(g * rows, rows) for g in range(groups)]
    halos = [far[at, :] + close[at, :] for at in places]
    firsts = [
        conv_blocks(
            jnp.concatenate([halo[:, :LANES], mixed[at, :]], axis=1), matrices_one[g], 0, 1
        )
        for g, (at, halo) in enumerate(zip(places, halos))
    ]
    firsts = [
        (gate_one[at, :].astype(F32) * first).astype(BF16) for at, first in zip(places, firsts)
    ]
    for g, (at, halo, first) in enumerate(zip(places, halos, firsts)):
        wide = jnp.concatenate([halo[:, LANES:], first, kept[at, :]], axis=1)
        second = conv_blocks(wide, matrices_two[g], 0, 2)
        out[at, : 2 * LANES] = (gate_two[at, :].astype(F32) * second).astype(BF16)
        if not SPLIT:
            out[at, 2 * LANES :] = refs[0][at, :]


def tables(length, devices):
    n = LANES
    per = length // n // devices
    order = np.arange(n)
    n1 = (order % devices) * per + order // devices
    k1 = np.arange(n) + 0.25
    outer = 2 * np.pi * np.outer(k1, n1) / n
    outer_table = np.concatenate([np.cos(outer), -np.sin(outer)], axis=0)
    inner = 2 * np.pi * np.outer(np.arange(n), np.arange(n)) / n
    cos, sin = np.cos(inner), np.sin(inner)
    ahead = np.block([[cos, -sin], [sin, cos]])
    back = np.block([[cos, sin], [-sin, cos]])
    turn = 2 * np.pi * np.outer(k1, np.arange(n)) / length
    half = lambda t: jnp.asarray(t, F32).astype(BF16)
    return (
        half(outer_table),
        half(outer_table.T),
        half(ahead),
        half(back),
        jnp.asarray(np.cos(turn), F32),
        jnp.asarray(np.sin(turn), F32),
    )


def gather_rows(rows, channel, channels):
    count = rows.shape[1] // channels
    picked = [rows[q, pl.ds(channel, count, stride=channels), :] for q in range(rows.shape[0])]
    return jnp.concatenate(picked, axis=0)


def side_by_side(signals):
    return jnp.concatenate([s.astype(BF16) for s in signals], axis=1)


def turn_ahead(parts, cos, sin):
    n = LANES
    turned = []
    for at in range(0, parts.shape[1], n):
        re, im = parts[:n, at : at + n], parts[n:, at : at + n]
        both = jnp.concatenate([re * cos + im * sin, im * cos - re * sin], axis=1)
        turned.append(both.astype(BF16))
    return jnp.concatenate(turned, axis=0)


def weigh(waves, spectra):
    n = LANES
    products = []
    for i, spectrum in enumerate(spectra):
        re, im = waves[i * n : (i + 1) * n, :n], waves[i * n : (i + 1) * n, n:]
        filter_re, filter_im = spectrum[:, :n], spectrum[:, n:]
        both = [re * filter_re - im * filter_im, re * filter_im + im * filter_re]
        products.append(jnp.concatenate(both, axis=1).astype(BF16))
    return jnp.concatenate(products, axis=0)


def turn_back(waves, cos, sin):
    n = LANES
    turned = []
    for at in range(0, waves.shape[0], n):
        re, im = waves[at : at + n, :n], waves[at : at + n, n:]
        both = [re * cos - im * sin, re * sin + im * cos]
        turned.append(jnp.concatenate(both, axis=0).astype(BF16))
    return jnp.concatenate(turned, axis=1)


def filter_kernel(taps, outer, ahead, cos, sin, spectrum, rows):
    channels, length = taps.shape
    n = LANES
    per = rows.shape[0]
    for b in range(length // n):
        at = pl.ds(b // per * channels, channels)
        rows[b % per, at, :] = taps[:, b * n : (b + 1) * n].astype(F32)
    signals = [gather_rows(rows, c, channels) for c in range(channels)]
    waves = matmul(outer[...], side_by_side(signals))
    waves = matmul(turn_ahead(waves, cos[...], sin[...]), ahead[...])
    spectrum[...] = (waves * (1.0 / length)).reshape(spectrum.shape)


def long_kernel(*refs):
    if SPLIT:
        late, early, spectrum, skip, outer, outer_t, ahead, back, cos, sin, out, rows, outs = refs
    else:
        early, spectrum, skip, outer, outer_t, ahead, back, cos, sin, out, rows, outs = refs
    n = LANES
    devices, channels, length = out.shape
    for part, piece in enumerate((early, late) if SPLIT else (early,)):
        width = piece.shape[2]
        flat = piece[...].astype(F32).reshape(devices * channels, width)
        for q in range(width // n):
            rows[part * (width // n) + q] = flat[:, q * n : (q + 1) * n]
    base = lax.axis_index("ctx") * channels
    cosines, sines = cos[...], sin[...]
    batches = [range(c, c + BATCH) for c in range(0, channels, BATCH)]
    signals = [[gather_rows(rows, c, channels) for c in batch] for batch in batches]
    waves = [matmul(outer[...], side_by_side(s)) for s in signals]
    waves = [matmul(turn_ahead(w, cosines, sines), ahead[...]) for w in waves]
    waves = [
        matmul(weigh(w, [spectrum[c] for c in batch]), back[...])
        for w, batch in zip(waves, batches)
    ]
    waves = [matmul(outer_t[...], turn_back(w, cosines, sines)) for w in waves]
    for batch, signal, result in zip(batches, signals, waves):
        for i, c in enumerate(batch):
            block = result[:, i * n : (i + 1) * n] + skip[base + c] * signal[i]
            for q in range(length // n):
                at = pl.ds(c, devices, stride=channels)
                outs[q, at, :] = block[q * devices : (q + 1) * devices]
    for q in range(length // n):
        block = outs[q].reshape(devices, channels, n)
        out[:, :, q * n : (q + 1) * n] = block.astype(BF16)


def gate_kernel(gate, data, out, held, sems):
    rows = gate.shape[0] // PARTS
    copies = []
    for p in range(PARTS):
        at = pl.ds(p * rows, rows)
        held[p] = (gate[at, :].astype(F32) * data[at, :].astype(F32)).astype(BF16)
        copies.append(pltpu.make_async_copy(held.at[p], out.at[at, :], sems.at[p]))
        copies[-1].start()
    for copy in copies:
        copy.wait()


def shards(
    value_in,
    key_in,
    gate_first,
    gate_second,
    gate_long,
    filter_first,
    filter_second,
    long_filter,
    skip_gain,
):
    channels, length = value_in.shape
    devices = lax.axis_size("ctx")
    per = channels // devices
    groups = filter_first.shape[0]
    half = length // 2
    outer, outer_t, ahead, back, cos, sin = [near_core(t) for t in tables(length * devices, devices)]
    bands = pltpu.VMEM((groups, 2 * LANES, LANES), BF16)
    block = pltpu.VMEM((channels, LANES), BF16)
    pair = pltpu.VMEM((channels, 2 * LANES), BF16)
    value, key, gate_one, gate_two = map(in_hbm, (value_in, key_in, gate_first, gate_second))
    tails, ones = call(
        tail_kernel,
        (pair, bands),
        value,
        key,
        gate_one,
        in_hbm(filter_first),
        specs=[pl.BlockSpec(memory_space=pl.ANY)] * 4,
        scratch=[
            pair,
            pair,
            block,
            pltpu.VMEM(filter_first.shape, BF16),
            pltpu.SemaphoreType.DMA((4,)),
        ],
    )
    pairs = [(i, i + 1) for i in range(devices - 1)]
    far = lax.ppermute(tails, "ctx", [p for p in pairs if p[1] % ROW == 0])
    close = lax.ppermute(tails, "ctx", [p for p in pairs if p[1] % ROW])
    ones = near_core(ones)
    kept, late, twos, mixed, gate_one, gate_two = call(
        near_kernel,
        (block, pair, bands, block, block, pair),
        value,
        key,
        gate_one,
        gate_two,
        ones,
        in_hbm(filter_second),
        near_core(tails),
    )
    plane = pltpu.VMEM((length // LANES, devices * per, LANES), F32)
    spectrum = call(
        filter_kernel,
        pltpu.VMEM((per, LANES, 2 * LANES), F32),
        near_core(long_filter),
        outer,
        ahead,
        cos,
        sin,
        scratch=[plane],
    )
    kept, spectrum = lax.optimization_barrier((kept, spectrum))
    mixed, gate_one, gate_two = map(near_core, (mixed, gate_one, gate_two))
    width = half if SPLIT else length
    rest = () if SPLIT else (near_core(late),)
    early = call(
        edge_kernel,
        pltpu.VMEM((channels, width), BF16),
        mixed,
        gate_one,
        gate_two,
        near_core(kept),
        ones,
        near_core(twos),
        near_core(far),
        near_core(close),
        *rest,
    )

    def swap(data):
        return lax.all_to_all(data, "ctx", split_axis=0, concat_axis=0, tiled=True)

    moved = [swap(early.reshape(devices, per, width))]
    if SPLIT:
        moved = [swap(late.reshape(devices, per, half))] + moved
    long_out = call(
        long_kernel,
        pltpu.VMEM((devices, per, length), BF16),
        *map(near_core, moved),
        near_core(spectrum),
        skip_gain,
        outer,
        outer_t,
        ahead,
        back,
        cos,
        sin,
        specs=[VMEM] * (len(moved) + 1) + [SMEM] + [VMEM] * 6,
        scratch=[plane, plane],
    )
    back_home = swap(long_out).reshape(channels, length)
    return pl.pallas_call(
        gate_kernel,
        out_shape=jax.ShapeDtypeStruct((channels, length), BF16),
        in_specs=[VMEM, VMEM],
        out_specs=pl.BlockSpec(memory_space=pl.ANY),
        scratch_shapes=[
            pltpu.VMEM((PARTS, channels // PARTS, length), BF16),
            pltpu.SemaphoreType.DMA((PARTS,)),
        ],
        compiler_params=pltpu.CompilerParams(vmem_limit_bytes=16 << 20),
        name="gate",
    )(near_core(gate_long), near_core(back_home))


def solution(mesh):
    placed = (
        P("ch", "ctx"),
        P("ch", "ctx"),
        P("ch", "ctx"),
        P("ch", "ctx"),
        P("ch", "ctx"),
        P("ch", None),
        P("ch", None),
        P(("ch", "ctx"), None),
        P("ch"),
    )
    return jax.shard_map(
        shards, mesh=mesh, in_specs=placed, out_specs=P("ch", "ctx"), check_vma=False
    )
```

```python
import jax
import jax.numpy as jnp
import numpy as np
from jax import lax
from jax.experimental import pallas as pl
from jax.experimental.pallas import tpu as pltpu
from jax.sharding import PartitionSpec as P


SPLIT = False
LANES = 128
ROW = 8
PARTS = 2
BATCH = 1
VMEM = pl.BlockSpec(memory_space=pltpu.VMEM)
SMEM = pl.BlockSpec(memory_space=pltpu.SMEM)
BF16 = jnp.bfloat16
F32 = jnp.float32


def near_core(data):
    return pltpu.with_memory_space_constraint(data, pltpu.VMEM)


def in_hbm(data):
    return pltpu.with_memory_space_constraint(data, pltpu.HBM)


def call(kernel, outs, *args, specs=None, scratch=()):
    return pl.pallas_call(
        kernel,
        out_shape=outs,
        grid=(1,),
        in_specs=specs or [VMEM] * len(args),
        out_specs=(VMEM,) * len(outs) if isinstance(outs, tuple) else VMEM,
        scratch_shapes=list(scratch),
        compiler_params=pltpu.CompilerParams(vmem_limit_bytes=16 << 20),
    )(*args)


def matmul(a, b):
    return jnp.dot(a, b, preferred_element_type=F32)


def band(taps_ref, group):
    taps = taps_ref[pl.ds(group, 1), :].astype(F32)
    ring = jnp.concatenate([taps, jnp.zeros_like(taps)], axis=1)
    rows = jnp.broadcast_to(ring, (8, 2 * LANES))
    rows = pltpu.roll(rows, LANES, 1, stride=1, stride_axis=0)
    strips = [rows if m == 0 else pltpu.roll(rows, 8 * m, 1) for m in range(LANES // 8)]
    top = jnp.concatenate([s[:, :LANES] for s in strips], axis=0)
    bottom = jnp.concatenate([s[:, LANES:] for s in strips], axis=0)
    return jnp.concatenate([top, bottom], axis=0).astype(BF16)


def conv_blocks(wide, matrix, first, last):
    rows = wide.shape[0]
    stack = jnp.concatenate(
        [wide[:, b * LANES : (b + 2) * LANES] for b in range(first, last)], axis=0
    )
    out = matmul(stack, matrix)
    return jnp.concatenate([out[i * rows : (i + 1) * rows] for i in range(last - first)], axis=1)


def tail_kernel(value, key, gate, taps, tails, matrices, values, keys, gates, held, sems):
    groups = taps.shape[0]
    rows, length = value.shape[0] // groups, value.shape[1]
    width = values.shape[1]
    copies = [
        pltpu.make_async_copy(source, target, sems.at[i])
        for i, (source, target) in enumerate(
            (
                (taps, held),
                (value.at[:, pl.ds(length - width, width)], values),
                (key.at[:, pl.ds(length - width, width)], keys),
                (gate.at[:, pl.ds(length - LANES, LANES)], gates),
            )
        )
    ]
    for copy in copies:
        copy.start()
    copies[0].wait()
    for g in range(groups // 4):
        matrices[g] = band(held, g)
    for copy in copies[1:]:
        copy.wait()
    for g in range(groups):
        at = pl.ds(g * rows, rows)
        if g >= groups // 4:
            matrices[g] = band(held, g)
        mixed = (keys[at, :].astype(F32) * values[at, :].astype(F32)).astype(BF16)
        tails[at, :LANES] = mixed[:, LANES:]
        first = conv_blocks(mixed, matrices[g], 0, 1)
        tails[at, LANES:] = (gates[at, :].astype(F32) * first).astype(BF16)


def near_kernel(
    value, key, gate_one, gate_two, ahead, taps, tails, kept, out, matrices, mixed, one, two
):
    groups = taps.shape[0]
    rows = value.shape[0] // groups
    half = 2 * LANES
    for g in range(groups):
        at = pl.ds(g * rows, rows)
        matrix = band(taps, g)
        matrices[g] = matrix
        block = key[at, : 3 * LANES].astype(F32) * value[at, : 3 * LANES].astype(F32)
        block = block.astype(BF16)
        mixed[at, :] = block[:, :LANES]
        first = conv_blocks(block, ahead[g], 0, 2)
        first = (gate_one[at, LANES : 3 * LANES].astype(F32) * first).astype(BF16)
        kept[at, :] = first[:, :LANES]
        first = jnp.concatenate([first, tails[at, LANES:]], axis=1)
        second = conv_blocks(first, matrix, 0, 2)
        out[at, :] = (gate_two[at, half:].astype(F32) * second).astype(BF16)
    one[...] = gate_one[:, :LANES]
    two[...] = gate_two[:, :half]


def edge_kernel(mixed, gate_one, gate_two, kept, matrices_one, matrices_two, far, close, *refs):
    out = refs[-1]
    groups = matrices_one.shape[0]
    rows = mixed.shape[0] // groups
    for g in range(groups):
        at = pl.ds(g * rows, rows)
        halo = far[at, :] + close[at, :]
        first = jnp.concatenate([halo[:, :LANES], mixed[at, :]], axis=1)
        first = conv_blocks(first, matrices_one[g], 0, 1)
        first = (gate_one[at, :].astype(F32) * first).astype(BF16)
        first = jnp.concatenate([halo[:, LANES:], first, kept[at, :]], axis=1)
        second = conv_blocks(first, matrices_two[g], 0, 2)
        out[at, : 2 * LANES] = (gate_two[at, :].astype(F32) * second).astype(BF16)
        if not SPLIT:
            out[at, 2 * LANES :] = refs[0][at, :]


def tables(length, devices):
    n = LANES
    per = length // n // devices
    order = np.arange(n)
    n1 = (order % devices) * per + order // devices
    k1 = np.arange(n) + 0.25
    outer = 2 * np.pi * np.outer(k1, n1) / n
    outer_table = np.concatenate([np.cos(outer), -np.sin(outer)], axis=0)
    inner = 2 * np.pi * np.outer(np.arange(n), np.arange(n)) / n
    cos, sin = np.cos(inner), np.sin(inner)
    ahead = np.block([[cos, -sin], [sin, cos]])
    back = np.block([[cos, sin], [-sin, cos]])
    turn = 2 * np.pi * np.outer(k1, np.arange(n)) / length
    half = lambda t: jnp.asarray(t, F32).astype(BF16)
    return (
        half(outer_table),
        half(outer_table.T),
        half(ahead),
        half(back),
        jnp.asarray(np.cos(turn), F32),
        jnp.asarray(np.sin(turn), F32),
    )


def gather_rows(rows, channel, channels):
    count = rows.shape[1] // channels
    picked = [rows[q, pl.ds(channel, count, stride=channels), :] for q in range(rows.shape[0])]
    return jnp.concatenate(picked, axis=0)


def side_by_side(signals):
    return jnp.concatenate([s.astype(BF16) for s in signals], axis=1)


def turn_ahead(parts, cos, sin):
    n = LANES
    turned = []
    for at in range(0, parts.shape[1], n):
        re, im = parts[:n, at : at + n], parts[n:, at : at + n]
        both = jnp.concatenate([re * cos + im * sin, im * cos - re * sin], axis=1)
        turned.append(both.astype(BF16))
    return jnp.concatenate(turned, axis=0)


def weigh(waves, spectra):
    n = LANES
    products = []
    for i, spectrum in enumerate(spectra):
        re, im = waves[i * n : (i + 1) * n, :n], waves[i * n : (i + 1) * n, n:]
        filter_re, filter_im = spectrum[:, :n], spectrum[:, n:]
        both = [re * filter_re - im * filter_im, re * filter_im + im * filter_re]
        products.append(jnp.concatenate(both, axis=1).astype(BF16))
    return jnp.concatenate(products, axis=0)


def turn_back(waves, cos, sin):
    n = LANES
    turned = []
    for at in range(0, waves.shape[0], n):
        re, im = waves[at : at + n, :n], waves[at : at + n, n:]
        both = [re * cos - im * sin, re * sin + im * cos]
        turned.append(jnp.concatenate(both, axis=0).astype(BF16))
    return jnp.concatenate(turned, axis=1)


def filter_kernel(taps, outer, ahead, cos, sin, spectrum, rows):
    channels, length = taps.shape
    n = LANES
    per = rows.shape[0]
    for b in range(length // n):
        at = pl.ds(b // per * channels, channels)
        rows[b % per, at, :] = taps[:, b * n : (b + 1) * n].astype(F32)
    signals = [gather_rows(rows, c, channels) for c in range(channels)]
    waves = matmul(outer[...], side_by_side(signals))
    waves = matmul(turn_ahead(waves, cos[...], sin[...]), ahead[...])
    spectrum[...] = (waves * (1.0 / length)).reshape(spectrum.shape)


def long_kernel(*refs):
    if SPLIT:
        late, early, spectrum, skip, outer, outer_t, ahead, back, cos, sin, out, rows, outs = refs
    else:
        early, spectrum, skip, outer, outer_t, ahead, back, cos, sin, out, rows, outs = refs
    n = LANES
    devices, channels, length = out.shape
    for part, piece in enumerate((early, late) if SPLIT else (early,)):
        width = piece.shape[2]
        flat = piece[...].astype(F32).reshape(devices * channels, width)
        for q in range(width // n):
            rows[part * (width // n) + q] = flat[:, q * n : (q + 1) * n]
    base = lax.axis_index("ctx") * channels
    cosines, sines = cos[...], sin[...]
    batches = [range(c, c + BATCH) for c in range(0, channels, BATCH)]
    signals = [[gather_rows(rows, c, channels) for c in batch] for batch in batches]
    waves = [matmul(outer[...], side_by_side(s)) for s in signals]
    waves = [matmul(turn_ahead(w, cosines, sines), ahead[...]) for w in waves]
    waves = [
        matmul(weigh(w, [spectrum[c] for c in batch]), back[...])
        for w, batch in zip(waves, batches)
    ]
    waves = [matmul(outer_t[...], turn_back(w, cosines, sines)) for w in waves]
    for batch, signal, result in zip(batches, signals, waves):
        for i, c in enumerate(batch):
            block = result[:, i * n : (i + 1) * n] + skip[base + c] * signal[i]
            for q in range(length // n):
                at = pl.ds(c, devices, stride=channels)
                outs[q, at, :] = block[q * devices : (q + 1) * devices]
    for q in range(length // n):
        block = outs[q].reshape(devices, channels, n)
        out[:, :, q * n : (q + 1) * n] = block.astype(BF16)


def gate_kernel(gate, data, out, held, sems):
    rows = gate.shape[0] // PARTS
    copies = []
    for p in range(PARTS):
        at = pl.ds(p * rows, rows)
        held[p] = (gate[at, :].astype(F32) * data[at, :].astype(F32)).astype(BF16)
        copies.append(pltpu.make_async_copy(held.at[p], out.at[at, :], sems.at[p]))
        copies[-1].start()
    for copy in copies:
        copy.wait()


def shards(
    value_in,
    key_in,
    gate_first,
    gate_second,
    gate_long,
    filter_first,
    filter_second,
    long_filter,
    skip_gain,
):
    channels, length = value_in.shape
    devices = lax.axis_size("ctx")
    per = channels // devices
    groups = filter_first.shape[0]
    half = length // 2
    outer, outer_t, ahead, back, cos, sin = [near_core(t) for t in tables(length * devices, devices)]
    bands = pltpu.VMEM((groups, 2 * LANES, LANES), BF16)
    block = pltpu.VMEM((channels, LANES), BF16)
    pair = pltpu.VMEM((channels, 2 * LANES), BF16)
    value, key, gate_one, gate_two = map(in_hbm, (value_in, key_in, gate_first, gate_second))
    tails, ones = call(
        tail_kernel,
        (pair, bands),
        value,
        key,
        gate_one,
        in_hbm(filter_first),
        specs=[pl.BlockSpec(memory_space=pl.ANY)] * 4,
        scratch=[
            pair,
            pair,
            block,
            pltpu.VMEM(filter_first.shape, BF16),
            pltpu.SemaphoreType.DMA((4,)),
        ],
    )
    pairs = [(i, i + 1) for i in range(devices - 1)]
    far = lax.ppermute(tails, "ctx", [p for p in pairs if p[1] % ROW == 0])
    close = lax.ppermute(tails, "ctx", [p for p in pairs if p[1] % ROW])
    ones = near_core(ones)
    kept, late, twos, mixed, gate_one, gate_two = call(
        near_kernel,
        (block, pair, bands, block, block, pair),
        value,
        key,
        gate_one,
        gate_two,
        ones,
        in_hbm(filter_second),
        near_core(tails),
    )
    plane = pltpu.VMEM((length // LANES, devices * per, LANES), F32)
    spectrum = call(
        filter_kernel,
        pltpu.VMEM((per, LANES, 2 * LANES), F32),
        near_core(long_filter),
        outer,
        ahead,
        cos,
        sin,
        scratch=[plane],
    )
    kept, spectrum = lax.optimization_barrier((kept, spectrum))
    mixed, gate_one, gate_two = map(near_core, (mixed, gate_one, gate_two))
    width = half if SPLIT else length
    rest = () if SPLIT else (near_core(late),)
    early = call(
        edge_kernel,
        pltpu.VMEM((channels, width), BF16),
        mixed,
        gate_one,
        gate_two,
        near_core(kept),
        ones,
        near_core(twos),
        near_core(far),
        near_core(close),
        *rest,
    )

    def swap(data):
        return lax.all_to_all(data, "ctx", split_axis=0, concat_axis=0, tiled=True)

    moved = [swap(early.reshape(devices, per, width))]
    if SPLIT:
        moved = [swap(late.reshape(devices, per, half))] + moved
    long_out = call(
        long_kernel,
        pltpu.VMEM((devices, per, length), BF16),
        *map(near_core, moved),
        near_core(spectrum),
        skip_gain,
        outer,
        outer_t,
        ahead,
        back,
        cos,
        sin,
        specs=[VMEM] * (len(moved) + 1) + [SMEM] + [VMEM] * 6,
        scratch=[plane, plane],
    )
    back_home = swap(long_out).reshape(channels, length)
    return pl.pallas_call(
        gate_kernel,
        out_shape=jax.ShapeDtypeStruct((channels, length), BF16),
        in_specs=[VMEM, VMEM],
        out_specs=pl.BlockSpec(memory_space=pl.ANY),
        scratch_shapes=[
            pltpu.VMEM((PARTS, channels // PARTS, length), BF16),
            pltpu.SemaphoreType.DMA((PARTS,)),
        ],
        compiler_params=pltpu.CompilerParams(vmem_limit_bytes=16 << 20),
        name="gate",
    )(near_core(gate_long), near_core(back_home))


def solution(mesh):
    placed = (
        P("ch", "ctx"),
        P("ch", "ctx"),
        P("ch", "ctx"),
        P("ch", "ctx"),
        P("ch", "ctx"),
        P("ch", None),
        P("ch", None),
        P(("ch", "ctx"), None),
        P("ch"),
    )
    return jax.shard_map(
        shards, mesh=mesh, in_specs=placed, out_specs=P("ch", "ctx"), check_vma=False
    )
```
